32 devices in a mesh: dp: 4 (over y, x), wide: 8 (over z, core).
Axes of the slice: x: 2, y: 2, z: 4, core: 2. Of those that a mesh axis runs over, the one named last changes fastest.
Arguments:
- clips: bfloat16 [4, 8, 4, 128, 512], P('dp', 'wide'), may hold values from -8 to 8
- w_spatial: bfloat16 [4608, 512], P(None, 'dp'), may hold values from -0.09375 to 0.09375
- w_time: bfloat16 [1536, 512], replicated, may hold values from -0.15625 to 0.15625
- norm_gain: float32 [512], replicated, may hold values from 0.1 to 1.9
- norm_bias: float32 [512], replicated, may hold values from -0.6 to 0.6
- grad_out: bfloat16 [4, 8, 512, 512], P('dp', None, 'wide'), may hold values from -6 to 6
Outputs:
- grad_clips: bfloat16 [4, 8, 4, 128, 512], P('dp', 'wide')
- spatial_grad: float32 [4608, 512], P('dp', 'wide')
- time_grad: float32 [1536, 512], P('dp', 'wide')
The draws below stay inside these ranges and needn't reach their ends.
All inputs are finite; a program needn't handle non-finite values.
Results may differ from the reference program's by a relative error of at most 0.009.
Values may be sent and summed in bfloat16 or wider, within the bound.
No kernel may reach another device: no remote copies, remote signals or barrier semaphores. Data moves between devices by JAX's collectives and lax.ppermute only.
A program may use at most 128 MiB of HBM per device.

```python
import jax
import jax.numpy as jnp
from jax import lax

C = 512
G = 32
HS = 4
WS = 128
FRAMES = 8
CL_GROUP = 1
CLIPS = 4
PIX = 512
N_DP = 4


def draw_clips(key, part):
    shape = (N_DP, CL_GROUP * FRAMES, HS, WS, C)
    noise = jax.random.normal(jax.random.fold_in(key, 11), shape, jnp.float32)
    values = noise
    return jnp.clip(values, -8.0, 8.0).astype(jnp.bfloat16)


def strengthened(entries, own_key, source, target, blocks, factor):
    owner, partner = [(jnp.arange(entries.shape[position]) // (entries.shape[position] // blocks)).reshape([-1 if axis == position else 1 for axis in range(entries.ndim)]) for position in (source, target)]
    chosen = jax.random.permutation(own_key, blocks)[partner]
    strong = (owner == chosen) | (owner == (partner + blocks // 2) % blocks)
    return jnp.where(strong, factor * entries, entries)


def steps_of(stream_key, extent, cuts, smallest, largest):
    factor_of = 1.0
    for position, shards_of in cuts:
        draws = jax.random.uniform(jax.random.fold_in(jax.random.fold_in(stream_key, 6), position), (shards_of,), jnp.float32, smallest / len(cuts), largest / len(cuts))
        factor_of = factor_of * jnp.repeat(jnp.exp(draws), extent[position] // shards_of).reshape((-1,) + (1,) * (len(extent) - 1 - position))
    return factor_of


def normal_values(rng, shape, spread, reach, pieces=(), held_as=jnp.bfloat16):
    result = spread * jax.random.normal(rng, shape, jnp.float32)
    if pieces:
        result = result * steps_of(rng, shape, pieces, -0.22, 0.18)
    return jnp.clip(result, -reach, reach).astype(held_as)


def gaussian_with(stream_key, dims, spread, most, shards, heavy, dtype=jnp.bfloat16):
    entries = spread * jax.random.normal(stream_key, dims, jnp.float32)
    if shards:
        entries = entries * steps_of(stream_key, dims, shards, -0.22, 0.18)
    return jnp.clip(strengthened(entries, jax.random.fold_in(stream_key, 3), *heavy), -most, most).astype(dtype)


def setup_inputs(seed: int = 0) -> dict:
    keys = jax.random.split(jax.random.key(seed), 7)
    clips = draw_clips(jax.random.fold_in(keys[6], 71), 0)
    w_spatial = normal_values(keys[1], (9 * C, C), (9 * C) ** -0.5, 0.09375, ((1, 4),))
    w_time = normal_values(keys[2], (3 * C, C), (3 * C) ** -0.5, 0.15625)
    norm_gain = jnp.clip(1.0 + 0.18 * jax.random.normal(keys[3], (C,), jnp.float32), 0.1, 1.9)
    norm_bias = jnp.clip(jax.random.uniform(keys[4], (C,), jnp.float32, -0.6, 0.6), -0.6, 0.6)
    grad_out = gaussian_with(keys[5], (N_DP, CL_GROUP * FRAMES, PIX, C), 1.0, 6.0, ((0, 4), (2, 8)), (2, 3, 8, 2.0))
    return {"clips": clips, "w_spatial": w_spatial, "w_time": w_time, "norm_gain": norm_gain, "norm_bias": norm_bias, "grad_out": grad_out}


EPSILON = 1e-06
CONTRACT_ROWS = (((0,), (0,)), ((), ()))
CONTRACT_COLS = (((1,), (1,)), ((), ()))

def pad_frames(frames):
    return jnp.pad(frames, ((0, 0), (1, 1), (1, 1), (0, 0)))

def spatial_forward(frames, weights):
    frame_total, row_count, col_count, chan_count = frames.shape
    padded = pad_frames(frames)
    accum_out = jnp.zeros((frame_total * row_count * col_count, weights.shape[1]), jnp.float32)
    for tap_index in range(9):
        row_off, col_off = (tap_index // 3, tap_index % 3)
        window = padded[:, row_off:row_off + row_count, col_off:col_off + col_count, :].reshape(-1, chan_count)
        tap_weight = weights[tap_index * chan_count:(tap_index + 1) * chan_count]
        accum_out = accum_out + jnp.dot(window, tap_weight, preferred_element_type=jnp.float32)
    return accum_out.reshape(frame_total, row_count, col_count, -1)

def spatial_backward(frames, grad_hidden, weights):
    frame_total, row_count, col_count, chan_count = frames.shape
    padded_in = pad_frames(frames)
    padded_grad = pad_frames(grad_hidden)
    grad_flat = grad_hidden.reshape(-1, chan_count)
    grad_input = jnp.zeros((frame_total * row_count * col_count, chan_count), jnp.float32)
    tap_grads = []
    for tap_index in range(9):
        row_off, col_off = (tap_index // 3, tap_index % 3)
        window = padded_in[:, row_off:row_off + row_count, col_off:col_off + col_count, :].reshape(-1, chan_count)
        tap_grads.append(lax.dot_general(window, grad_flat, CONTRACT_ROWS, preferred_element_type=jnp.float32))
        flipped = padded_grad[:, 2 - row_off:2 - row_off + row_count, 2 - col_off:2 - col_off + col_count, :].reshape(-1, chan_count)
        tap_weight = weights[tap_index * chan_count:(tap_index + 1) * chan_count]
        grad_input = grad_input + lax.dot_general(flipped, tap_weight, CONTRACT_COLS, preferred_element_type=jnp.float32)
    return (grad_input.reshape(frames.shape), jnp.concatenate(tap_grads, axis=0))

def norm_forward(hidden, norm_gain, norm_bias):
    frame_total, row_count, col_count, chan_count = hidden.shape
    grouped = hidden.astype(jnp.float32).reshape(frame_total, row_count * col_count, G, chan_count // G)
    group_mean = lax.optimization_barrier(jnp.mean(grouped, axis=(1, 3), keepdims=True))
    centered = grouped - group_mean
    variance = lax.optimization_barrier(jnp.mean(centered * centered, axis=(1, 3), keepdims=True))
    inv_std = lax.rsqrt(variance + EPSILON)
    normed = centered * inv_std
    preact = normed.reshape(hidden.shape) * norm_gain + norm_bias
    return (preact, normed, inv_std)

def norm_backward(grad_act, preact, normed, inv_std, norm_gain):
    sigmoid_z = jax.nn.sigmoid(preact)
    grad_pre = grad_act.astype(jnp.float32) * sigmoid_z * (1.0 + preact * (1.0 - sigmoid_z))
    grad_normed = (grad_pre * norm_gain).reshape(normed.shape)
    mean_grad = lax.optimization_barrier(jnp.mean(grad_normed, axis=(1, 3), keepdims=True))
    mean_proj = lax.optimization_barrier(jnp.mean(grad_normed * normed, axis=(1, 3), keepdims=True))
    return ((grad_normed - mean_grad - normed * mean_proj) * inv_std).reshape(preact.shape)

def temporal_backward(tiles, grad_out, w_time):
    clip_count, frame_total, pix_count, chan_count = tiles.shape
    grad_act = jnp.zeros(tiles.shape, jnp.float32)
    tap_grads = []
    for tap_index in range(3):
        kept = frame_total - tap_index
        earlier = tiles[:, :kept].reshape(-1, chan_count)
        later = grad_out[:, tap_index:].reshape(-1, chan_count)
        tap_grads.append(lax.dot_general(earlier, later, CONTRACT_ROWS, preferred_element_type=jnp.float32))
        tap_weight = w_time[tap_index * chan_count:(tap_index + 1) * chan_count]
        back_part = lax.dot_general(later, tap_weight, CONTRACT_COLS, preferred_element_type=jnp.float32)
        back_part = back_part.reshape(clip_count, kept, pix_count, chan_count)
        grad_act = grad_act + jnp.pad(back_part, ((0, 0), (0, tap_index), (0, 0), (0, 0)))
    return (jnp.concatenate(tap_grads, axis=0), grad_act)

def reference(clips, w_spatial, w_time, norm_gain, norm_bias, grad_out):
    frames = clips.reshape(-1, HS, WS, C)
    hidden = spatial_forward(frames, w_spatial).astype(jnp.bfloat16)
    preact, normed, inv_std = norm_forward(hidden, norm_gain, norm_bias)
    act = jax.nn.silu(preact).astype(jnp.bfloat16)
    tiles = act.reshape(CLIPS, FRAMES, HS * WS, C)
    time_raw, grad_act = temporal_backward(tiles, grad_out.reshape(CLIPS, FRAMES, HS * WS, C), w_time)
    grad_act = grad_act.astype(jnp.bfloat16).reshape(frames.shape)
    grad_hidden = norm_backward(grad_act, preact, normed, inv_std, norm_gain).astype(jnp.bfloat16)
    grad_input, spatial_raw = spatial_backward(frames, grad_hidden, w_spatial)
    grad_scale = float(CLIPS * FRAMES * HS * WS) ** (-0.5)
    return (grad_input.astype(jnp.bfloat16).reshape(clips.shape), spatial_raw * grad_scale, time_raw * grad_scale)
```

```python
import functools

import jax
import jax.numpy as jnp
from jax import lax
from jax.experimental import pallas as pl
from jax.experimental.pallas import tpu as pltpu
from jax.sharding import PartitionSpec as P

G = 32
FRAMES = 8
EPSILON = 1e-06
F32 = jnp.float32
BF16 = jnp.bfloat16
NT = (((1,), (1,)), ((), ()))


VM = pl.BlockSpec(memory_space=pltpu.VMEM)
ANY = pl.BlockSpec(memory_space=pl.ANY)


def dot(a, b):
    return jnp.dot(a, b, preferred_element_type=F32)


def dot_nt(a, b):
    return lax.dot_general(a, b, NT, preferred_element_type=F32)


def place():
    d = lax.axis_index("dp")
    w = lax.axis_index("wide")
    return d % 2, d // 2, w // 2, w % 2


def low_lanes(shape):
    return lax.broadcasted_iota(jnp.int32, shape, len(shape) - 1) < shape[-1] // 2


def swap(v):
    return pltpu.roll(v, v.shape[-1] // 2, v.ndim - 1)


def struct(shape, dtype):
    return jax.ShapeDtypeStruct(shape, dtype)


def pack_kernel(w_ref, top_ref, bot_ref):
    rows, lanes = w_ref.shape
    part = rows // 4
    _, _, _, c = place()
    low = low_lanes((part, lanes))
    for i, out in enumerate((top_ref, bot_ref)):
        first = w_ref[part * i : part * (i + 1), :].astype(F32)
        second = w_ref[rows // 2 + part * i : rows // 2 + part * (i + 1), :].astype(F32)
        even = jnp.where(low, first, swap(second))
        odd = jnp.where(low, swap(first), second)
        out[...] = jnp.where(c == 0, even, odd).astype(BF16)


def shifted(x, cols, by):
    if by == 0:
        return x
    total = x.shape[0]
    col = lax.broadcasted_iota(jnp.int32, x.shape, 0) % cols
    edge = cols - 1 if by > 0 else 0
    return jnp.where(col == edge, 0.0, pltpu.roll(x, (-by) % total, 0))


def shifted_lanes(x, cols, by):
    if by == 0:
        return x
    total = x.shape[1]
    col = lax.broadcasted_iota(jnp.int32, x.shape, 1) % cols
    edge = cols - 1 if by > 0 else 0
    return jnp.where(col == edge, 0.0, pltpu.roll(x, (-by) % total, 1))


def prep_kernel(own_ref, par_ref, x3_ref, xt_ref, *, cols):
    pix, chans = own_ref.shape
    for f, ref in enumerate((own_ref, par_ref)):
        x = ref[...].astype(F32)
        xt = x.T
        for b in range(3):
            lanes = slice(chans * b, chans * (b + 1))
            x3_ref[f, 0:cols, lanes] = jnp.zeros((cols, chans), BF16)
            x3_ref[f, cols + pix : 2 * cols + pix, lanes] = jnp.zeros((cols, chans), BF16)
            x3_ref[f, cols : cols + pix, lanes] = shifted(x, cols, b - 1).astype(BF16)
            xt_ref[f, b, :, 0:cols] = jnp.zeros((chans, cols), BF16)
            xt_ref[f, b, :, cols + pix : 2 * cols + pix] = jnp.zeros((chans, cols), BF16)
            xt_ref[f, b, :, cols : cols + pix] = shifted_lanes(xt, cols, b - 1).astype(BF16)


def gact_kernel(*refs, parts, offsets):
    pieces, wt_ref, gact_ref, gs_ref, g_s, w_s = (
        refs[:parts],
        refs[parts],
        refs[parts + 1],
        refs[parts + 2],
        refs[parts + 3],
        refs[parts + 4],
    )
    x, y, z, c = place()
    _, pix, chans = g_s.shape
    width = chans // 8
    for piece, offset in zip(pieces, offsets(z, c)):
        n = piece.shape[1]
        for f in range(4):
            if n == pix:
                g_s[f, :, :] = piece[f, :, :]
            else:
                g_s[f, pl.ds(pl.multiple_of(offset * n, n), n), :] = piece[f, :, :]

    @pl.when((2 * z) % FRAMES + 2 >= FRAMES)
    def _():
        g_s[2:4, :, :] = jnp.zeros((2, pix, chans), BF16)

    for k in range(3):
        for s in range(4):
            row = pl.multiple_of(k * chans + 2 * width * s + width * c, width)
            w_s[k, width * s : width * (s + 1), :] = wt_ref[pl.ds(row, width), :]
    for slot, base in enumerate((c, 1 - c)):
        acc = dot_nt(g_s[base], w_s[0])
        acc += dot_nt(g_s[base + 1], w_s[1])
        acc += dot_nt(g_s[base + 2], w_s[2])
        gact_ref[slot, :, :] = acc.astype(BF16)
    low = low_lanes((pix, 2 * width))
    for f in range(4):
        for t in range(2):
            t0 = g_s[f, :, 4 * width * t : 4 * width * t + 2 * width].astype(F32)
            t1 = g_s[f, :, 4 * width * t + 2 * width : 4 * width * (t + 1)].astype(F32)
            even = jnp.where(low, t0, swap(t1))
            odd = jnp.where(low, swap(t0), t1)
            gs_ref[f, :, 2 * width * t : 2 * width * (t + 1)] = jnp.where(c == 0, even, odd).astype(BF16)


def group_mean(colsum, pix, group):
    n = colsum.shape[1]
    a = lax.broadcasted_iota(jnp.int32, (n, n), 0) // group
    b = lax.broadcasted_iota(jnp.int32, (n, n), 1) // group
    same = jnp.where(a == b, 1.0 / (pix * group), 0.0).astype(F32)
    wide = jnp.broadcast_to(colsum, (8, n))
    return jnp.dot(wide, same, preferred_element_type=F32, precision=lax.Precision.HIGHEST)[0:1]


def main_kernel(
    own_t, own_b, x_t, x_b, y_t, y_b, d_t, d_b, x3_ref, gact_ref, gain_ref, bias_ref, gh_ref, act_ref, ws_ref, *, cols, group
):
    x, y, _, _ = place()
    part, lanes = own_t.shape
    low = low_lanes((part, lanes))
    for i, packs in enumerate(((own_t, x_t, y_t, d_t), (own_b, x_b, y_b, d_b))):
        for t in range(2):
            near, far = packs[2 * t][...].astype(F32), packs[2 * t + 1][...].astype(F32)
            p0 = jnp.where(x == 0, near, far)
            p1 = jnp.where(x == 0, far, near)
            tile = pl.ds(pl.multiple_of(lanes * (y ^ t), lanes), lanes)
            ws_ref[part * i : part * (i + 1), tile] = jnp.where(low, p0, swap(p1)).astype(BF16)
            ws_ref[part * (2 + i) : part * (3 + i), tile] = jnp.where(low, swap(p0), p1).astype(BF16)
    pix = gact_ref.shape[1]
    deep = x3_ref.shape[2]
    gain, bias = gain_ref[...], bias_ref[...]
    for f in range(2):
        acc = dot(x3_ref[f, 0:pix, :], ws_ref[0:deep, :])
        for a in (1, 2):
            acc += dot(x3_ref[f, cols * a : cols * a + pix, :], ws_ref[deep * a : deep * (a + 1), :])
        hidden = acc.astype(BF16).astype(F32)
        mean = group_mean(jnp.sum(hidden, axis=0, keepdims=True), pix, group)
        centered = hidden - mean
        variance = group_mean(jnp.sum(centered * centered, axis=0, keepdims=True), pix, group)
        inv_std = lax.rsqrt(variance + EPSILON)
        normed = centered * inv_std
        preact = normed * gain + bias
        sig = jax.nn.sigmoid(preact)
        act_ref[f, :, :] = (preact * sig).T.astype(BF16)
        grad_pre = gact_ref[f].astype(F32) * sig * (1.0 + preact * (1.0 - sig))
        grad_normed = grad_pre * gain
        mean_grad = group_mean(jnp.sum(grad_normed, axis=0, keepdims=True), pix, group)
        mean_proj = group_mean(jnp.sum(grad_normed * normed, axis=0, keepdims=True), pix, group)
        gh_ref[f, :, :] = ((grad_normed - mean_grad - normed * mean_proj) * inv_std).astype(BF16)


def send_out(scratch, outs, sem, x, y):
    a_keep, a_send, b_keep, b_send = outs
    half = a_keep.shape[2]
    plan = []
    for t in range(2):
        plan.append((a_send.at[t], (x ^ 1) + 2 * (y ^ t), 0))
        plan.append((b_send.at[t], (x ^ t) + 2 * (y ^ 1), 1))
    for t in range(2):
        plan.append((a_keep.at[t], x + 2 * (y ^ t), 0))
        plan.append((b_keep.at[t], (x ^ t) + 2 * y, 1))
    copies = []
    for n, (dst, quarter, side) in enumerate(plan):
        copies.append(pltpu.make_async_copy(scratch.at[side, quarter], dst, sem.at[n]))
        copies[-1].start()
    for copy in copies:
        copy.wait()


def spatial_kernel(xt_ref, gh_ref, ak, asend, bk, bsend, p_s, sem, *, cols):
    x, y, _, _ = place()
    _, pix, width = gh_ref.shape
    chans = xt_ref.shape[2]
    quarter = p_s.shape[2]
    unit = 128
    for a in range(3):
        for b in range(3):
            acc = dot(xt_ref[0, b, :, cols * a : cols * a + pix], gh_ref[0])
            acc += dot(xt_ref[1, b, :, cols * a : cols * a + pix], gh_ref[1])
            for j in range(chans // unit):
                row = (3 * a + b) * chans + unit * j
                q, r = divmod(row, quarter)
                block = acc[unit * j : unit * (j + 1)].astype(BF16)
                p_s[0, q, r : r + unit, :] = block[:, : width // 2]
                p_s[1, q, r : r + unit, :] = block[:, width // 2 :]
    send_out(p_s, (ak, asend, bk, bsend), sem, x, y)


def time_kernel(own_ref, par_ref, gs_ref, ak, asend, bk, bsend, p_s, sem):
    x, y, _, c = place()
    _, half, pix = own_ref.shape
    width = gs_ref.shape[2]
    quarter = p_s.shape[2]
    block = half // 4
    for k in range(3):
        for other, ref in enumerate((own_ref, par_ref)):
            acc = dot(ref[other], gs_ref[c + k])
            acc += dot(ref[1 - other], gs_ref[1 - c + k])
            side = c ^ other
            for s in range(4):
                q, r = divmod(k * 2 * half + 2 * block * s, quarter)
                rows = pl.ds(pl.multiple_of(r + block * side, block), block)
                v = acc[block * s : block * (s + 1)].astype(BF16)
                p_s[0, q, rows, :] = v[:, : width // 2]
                p_s[1, q, rows, :] = v[:, width // 2 :]
    send_out(p_s, (ak, asend, bk, bsend), sem, x, y)


def fold_kernel(ak, ra, r2a, bk, rb, r2b, *refs):
    outs, v_s = refs[:4], refs[4]
    _, _, z, _ = place()
    rows = ak.shape[1]
    h = rows // 2
    low = low_lanes((h, ak.shape[2]))
    for t, (k, r, r2) in enumerate(((ak, ra, r2a), (bk, rb, r2b))):
        top, bot = (
            k[0, rr, :].astype(F32) + r[0, rr, :].astype(F32) + r2[rr, :].astype(F32) for rr in (slice(0, h), slice(h, rows))
        )
        v_s[2 * t] = jnp.where(low, top, swap(bot)).astype(BF16)
        v_s[2 * t + 1] = jnp.where(low, swap(top), bot).astype(BF16)
    for s, out in enumerate(outs):
        out[...] = v_s[z ^ s]


def last_kernel(a, b, c, d, out_ref, *, scale):
    total = (a[...].astype(F32) + b[...].astype(F32) + c[...].astype(F32) + d[...].astype(F32)) * scale
    h, lanes = total.shape
    out_ref[0:h, :] = total[:, : lanes // 2]
    out_ref[h:, :] = swap(total)[:, : lanes // 2]


def clips_kernel(gh_ref, ws_ref, own_ref, par_ref, y_s, *, cols):
    _, pix, width = gh_ref.shape
    chans = own_ref.shape[1]
    for f, out in enumerate((own_ref, par_ref)):
        gh = gh_ref[f].astype(F32)
        for b in range(3):
            y_s[b, 0:cols, :] = jnp.zeros((cols, width), BF16)
            y_s[b, cols + pix :, :] = jnp.zeros((cols, width), BF16)
            y_s[b, cols : cols + pix, :] = shifted(gh, cols, 1 - b).astype(BF16)
        acc = None
        for a in range(3):
            for b in range(3):
                tap = 3 * a + b
                part = dot_nt(y_s[b, cols * (2 - a) : cols * (2 - a) + pix, :], ws_ref[chans * tap : chans * (tap + 1), :])
                acc = part if acc is None else acc + part
        out[...] = acc


def call(kernel, outs, *args, out_specs=None, scratch=(), name=None):
    return pl.pallas_call(
        kernel,
        out_shape=outs,
        in_specs=[VM] * len(args),
        out_specs=out_specs if out_specs is not None else jax.tree.map(lambda _: VM, outs),
        scratch_shapes=list(scratch),
        name=name,
    )(*args)


def send_dp(v, s):
    return lax.ppermute(v, "dp", [(i, i ^ s) for i in range(lax.axis_size("dp"))])


def send_wide(v, s):
    return lax.ppermute(v, "wide", [(i, i ^ s) for i in range(lax.axis_size("wide"))])


def z_groups():
    n = lax.axis_size("wide")
    return [list(range(0, n, 2)), list(range(1, n, 2))]


def shards(clips, w_spatial, w_time, norm_gain, norm_bias, grad_out):
    group_count, frame_count, rows, cols, chans = clips.shape
    n_dp, n_wide = lax.axis_size("dp"), lax.axis_size("wide")
    chips = n_wide // 2
    assert group_count == 1 and frame_count == 1 and n_dp == 4
    pix = rows * cols
    half = chans // 2
    width = half // 4
    taps_rows = w_spatial.shape[0]
    _, frame_total, pix_here, _ = grad_out.shape
    d = lax.axis_index("dp")
    w = lax.axis_index("wide")
    z, c = w // 2, w % 2

    pack = struct((taps_rows // 4, 2 * width), BF16)
    own_t, own_b = call(pack_kernel, (pack, pack), w_spatial, name="pack")
    x_t, y_b = send_dp(own_t, 1), send_dp(own_b, 2)
    x_b, y_t = send_dp(own_b, 1), send_dp(own_t, 2)
    d_t, d_b = send_dp(x_t, 2), send_dp(y_b, 1)

    own_clips = clips.reshape(pix, chans)
    par_clips = send_wide(own_clips, 1)

    go = jnp.pad(grad_out[0], ((0, 2), (0, 0), (0, 0)))
    small = chips <= 4
    if small:
        own_go = [lax.dynamic_slice_in_dim(go, 2 * (z ^ s), 4, 0) for s in range(chips)]
        own_go = [own_go[0]] + [send_wide(own_go[s], 2 * s) for s in range(1, chips)]
        par_go = [send_wide(v, 1) for v in own_go]
        pieces = own_go + par_go

        def offsets(z, c):
            return [2 * (z ^ s) + c for s in range(chips)] + [2 * (z ^ s) + 1 - c for s in range(chips)]

    else:
        by_chip = [go[k : k + frame_total].reshape(chips, 2, pix_here, chans) for k in (0, 2)]
        mine = lax.all_to_all(
            jnp.concatenate(by_chip, axis=1), "wide", 0, 0, tiled=True, axis_index_groups=z_groups()
        )
        other = send_wide(mine, 1)
        pair = jnp.stack([jnp.where(c == 0, mine, other), jnp.where(c == 0, other, mine)], axis=1)
        pieces = [pair.transpose(2, 0, 1, 3, 4).reshape(4, pix, chans)]

        def offsets(z, c):
            return [0]

    frames_half = struct((2, pix, half), BF16)
    gact, gs = call(
        functools.partial(gact_kernel, parts=len(pieces), offsets=offsets),
        (frames_half, struct((4, pix, half), BF16)),
        *pieces,
        w_time,
        scratch=(pltpu.VMEM((4, pix, chans), BF16), pltpu.VMEM((3, half, chans), BF16)),
        name="gact",
    )
    x3, xt = call(
        functools.partial(prep_kernel, cols=cols),
        (struct((2, pix + 2 * cols, 3 * chans), BF16), struct((2, 3, chans, pix + 2 * cols), BF16)),
        own_clips,
        par_clips,
        name="prep",
    )
    gain = norm_gain.reshape(n_dp, 2, width)
    bias = norm_bias.reshape(n_dp, 2, width)
    gain, bias = (lax.dynamic_index_in_dim(v, c, 1).reshape(1, half) for v in (gain, bias))
    gh, act, ws = call(
        functools.partial(main_kernel, cols=cols, group=chans // G),
        (frames_half, struct((2, half, pix), BF16), struct((taps_rows, half), BF16)),
        *(own_t, own_b, x_t, x_b, y_t, y_b, d_t, d_b, x3, gact, gain, bias),
        name="main",
    )

    def partials(kernel, row_count, name, *args):
        quarter = row_count // n_dp
        out = struct((2, quarter, half // 2), BF16)
        return call(
            kernel,
            (out,) * 4,
            *args,
            out_specs=(ANY,) * 4,
            scratch=(pltpu.VMEM((2, n_dp, quarter, half // 2), BF16), pltpu.SemaphoreType.DMA((8,))),
            name=name,
        )

    def reduce_dp(parts):
        a_keep, a_send, b_keep, b_send = parts
        ra, rb = send_dp(a_send, 1), send_dp(b_send, 2)
        next_a = (a_keep[1].astype(F32) + ra[1].astype(F32)).astype(BF16)
        next_b = (b_keep[1].astype(F32) + rb[1].astype(F32)).astype(BF16)
        return a_keep, ra, send_dp(next_a, 2), b_keep, rb, send_dp(next_b, 1)

    position_total = group_count * frame_count * pix * n_wide * n_dp
    grad_scale = float(position_total) ** (-0.5)

    def reduce_z(parts):
        a_keep, ra, r2a, b_keep, rb, r2b = parts
        quarter = r2a.shape[0]
        if small and chips == 4:
            chunk = struct((quarter // 2, 2 * width), BF16)
            chunks = call(
                fold_kernel, (chunk,) * 4, *parts, scratch=(pltpu.VMEM((4, quarter // 2, 2 * width), BF16),), name="fold"
            )
            got = [chunks[0]] + [send_wide(chunks[s], 2 * s) for s in range(1, 4)]
            return call(
                functools.partial(last_kernel, scale=grad_scale), struct((quarter, width), F32), *got, name="last"
            )
        total = jnp.concatenate(
            [k[0].astype(F32) + r[0].astype(F32) + r2.astype(F32) for k, r, r2 in ((a_keep, ra, r2a), (b_keep, rb, r2b))],
            axis=1,
        )
        size = half // chips
        chunks = total.astype(BF16).reshape(quarter, chips, size).transpose(1, 0, 2)
        got = lax.all_to_all(chunks, "wide", 0, 0, tiled=True, axis_index_groups=z_groups())
        mine = jnp.sum(got.astype(F32), axis=0) * grad_scale
        moves = []
        for src in range(n_wide):
            s, i = divmod((src // 2) * size, width)
            moves.append((src, (2 * width * s + width * (src % 2) + i) // size))
        return lax.ppermute(mine, "wide", moves)

    spatial = reduce_dp(
        partials(functools.partial(spatial_kernel, cols=cols), taps_rows, "spatial", xt, gh)
    )
    par_act = send_wide(act, 1)
    timed = reduce_dp(partials(time_kernel, w_time.shape[0], "time", act, par_act, gs))
    image = struct((pix, chans), F32)
    own_grad, par_grad = call(
        functools.partial(clips_kernel, cols=cols),
        (image, image),
        gh,
        ws,
        scratch=(pltpu.VMEM((3, pix + 2 * cols, half), BF16),),
        name="clips",
    )
    grad_clips = (own_grad + send_wide(par_grad, 1)).astype(BF16).reshape(clips.shape)
    return grad_clips, reduce_z(spatial), reduce_z(timed)


def solution(mesh):
    return jax.shard_map(
        shards,
        mesh=mesh,
        in_specs=(
            P("dp", "wide", None, None, None),
            P(None, "dp"),
            P(),
            P(),
            P(),
            P("dp", None, "wide", None),
        ),
        out_specs=(P("dp", "wide", None, None, None), P("dp", "wide"), P("dp", "wide")),
        check_vma=False,
    )
```

```python
import functools

import jax
import jax.numpy as jnp
from jax import lax
from jax.experimental import pallas as pl
from jax.experimental.pallas import tpu as pltpu
from jax.sharding import PartitionSpec as P

G = 32
FRAMES = 8
EPSILON = 1e-06
F32 = jnp.float32
BF16 = jnp.bfloat16
NT = (((1,), (1,)), ((), ()))


VM = pl.BlockSpec(memory_space=pltpu.VMEM)
PIECES = 2
SCOPED = 16 * 1024 * 1024


def dot(a, b):
    return jnp.dot(a, b, preferred_element_type=F32)


def dot_nt(a, b):
    return lax.dot_general(a, b, NT, preferred_element_type=F32)


def place():
    d = lax.axis_index("dp")
    w = lax.axis_index("wide")
    return d % 2, d // 2, w // 2, w % 2


def low_lanes(shape):
    return lax.broadcasted_iota(jnp.int32, shape, len(shape) - 1) < shape[-1] // 2


def swap(v):
    return pltpu.roll(v, v.shape[-1] // 2, v.ndim - 1)


def struct(shape, dtype):
    return jax.ShapeDtypeStruct(shape, dtype)


def pack_kernel(w_ref, top_ref, bot_ref):
    rows, lanes = w_ref.shape
    part = rows // 4
    _, _, _, c = place()
    low = low_lanes((part, lanes))
    for i, out in enumerate((top_ref, bot_ref)):
        first = w_ref[part * i : part * (i + 1), :].astype(F32)
        second = w_ref[rows // 2 + part * i : rows // 2 + part * (i + 1), :].astype(F32)
        even = jnp.where(low, first, swap(second))
        odd = jnp.where(low, swap(first), second)
        out[...] = jnp.where(c == 0, even, odd).astype(BF16)


def shifted(x, cols, by, axis=0):
    if by == 0:
        return x
    total = x.shape[axis]
    col = lax.broadcasted_iota(jnp.int32, x.shape, axis) % cols
    edge = cols - 1 if by > 0 else 0
    return jnp.where(col == edge, 0.0, pltpu.roll(x, (-by) % total, axis))


def prep_kernel(own_ref, par_ref, x3_ref, xt_ref, *, cols):
    pix, chans = own_ref.shape
    for f, ref in enumerate((own_ref, par_ref)):
        x = ref[...].astype(F32)
        xt = x.T
        for b in range(3):
            lanes = slice(chans * b, chans * (b + 1))
            x3_ref[f, 0:cols, lanes] = jnp.zeros((cols, chans), BF16)
            x3_ref[f, cols + pix : 2 * cols + pix, lanes] = jnp.zeros((cols, chans), BF16)
            x3_ref[f, cols : cols + pix, lanes] = shifted(x, cols, b - 1).astype(BF16)
            xt_ref[f, b, :, 0:cols] = jnp.zeros((chans, cols), BF16)
            xt_ref[f, b, :, cols + pix : 2 * cols + pix] = jnp.zeros((chans, cols), BF16)
            xt_ref[f, b, :, cols : cols + pix] = shifted(xt, cols, b - 1, 1).astype(BF16)


def gact_kernel(*refs, parts, pixels, chips):
    pieces, wt_ref, outs, g_ref, w_s, acc_s = refs[:parts], refs[parts], refs[parts + 1 : -3], refs[-3], refs[-2], refs[-1]
    _, _, z, c = place()
    total, chans = g_ref.shape
    frames = total // pixels
    width = chans // 8
    if parts == 1:
        g_ref[...] = pieces[0][...].reshape(total, chans)
    else:
        n = pixels // 2
        for piece, core in zip(pieces, (c, 1 - c)):
            for f in range(frames):
                g_ref[pl.ds(pl.multiple_of(pixels * f + n * core, n), n), :] = piece[f, :, :]
    for k in range(3):
        for s in range(4):
            row = pl.multiple_of(k * chans + 2 * width * s + width * c, width)
            w_s[k, width * s : width * (s + 1), :] = wt_ref[pl.ds(row, width), :]
    clip = FRAMES * pixels
    for base in range(0, total, clip):
        acc_s[base : base + clip, :] = dot_nt(g_ref[base : base + clip, :], w_s[0])
        for k in (1, 2):
            kept = clip - k * pixels
            acc_s[base : base + kept, :] += dot_nt(g_ref[base + k * pixels : base + clip, :], w_s[k])
    if len(outs) == 1:
        outs[0][...] = acc_s[...].astype(BF16)
    else:
        for s, out in enumerate(outs):
            rows = pl.multiple_of(2 * pixels * (z ^ s), 2 * pixels)
            out[...] = acc_s[pl.ds(rows, 2 * pixels), :].astype(BF16)


def group_mean(sums, pix, group):
    lane = lax.broadcasted_iota(jnp.int32, sums.shape, 1)
    total = sums.shape[1]
    step = 1
    while step < group:
        up = pltpu.roll(sums, total - step, 1)
        down = pltpu.roll(sums, step, 1)
        sums = sums + jnp.where((lane // step) % 2 == 0, up, down)
        step *= 2
    return sums * (1.0 / (pix * group))


def over_pixels(v):
    return jnp.sum(v, axis=0, keepdims=True)


def main_kernel(*refs, cols, group, parts):
    packs_t, packs_b, x3_ref = refs[0:4], refs[4:8], refs[8]
    pieces = refs[9 : 9 + parts]
    gain_ref, bias_ref, gh_ref, ws_ref = refs[9 + parts : 13 + parts]
    act_refs = refs[13 + parts : -3]
    ga_s, h_s, act_s = refs[-3:]
    x, y, z, c = place()
    part, lanes = packs_t[0].shape
    low = low_lanes((part, lanes))
    for i, packs in enumerate((packs_t, packs_b)):
        for t in range(2):
            near, far = packs[2 * t][...].astype(F32), packs[2 * t + 1][...].astype(F32)
            p0 = jnp.where(x == 0, near, far)
            p1 = jnp.where(x == 0, far, near)
            tile = pl.ds(pl.multiple_of(lanes * (y ^ t), lanes), lanes)
            ws_ref[part * i : part * (i + 1), tile] = jnp.where(low, p0, swap(p1)).astype(BF16)
            ws_ref[part * (2 + i) : part * (3 + i), tile] = jnp.where(low, swap(p0), p1).astype(BF16)
    _, pix, width = ga_s.shape
    deep = x3_ref.shape[2]
    gain, bias = gain_ref[...], bias_ref[...]
    order = (c, 1 - c)
    for f in range(2):
        acc = dot(x3_ref[f, 0:pix, :], ws_ref[0:deep, :])
        for a in (1, 2):
            acc += dot(x3_ref[f, cols * a : cols * a + pix, :], ws_ref[deep * a : deep * (a + 1), :])
        h_s[f, :, :] = acc.astype(BF16)
    for f in range(2):
        if parts == 1:
            ga_s[f, :, :] = pieces[0][order[f]]
        else:
            n = pix // parts
            for s, piece in enumerate(pieces):
                ga_s[f, pl.ds(pl.multiple_of(n * (z ^ s), n), n), :] = piece[pl.ds(pl.multiple_of(n * order[f], n), n), :]
    hidden = [h_s[f].astype(F32) for f in range(2)]
    mean = group_mean(jnp.concatenate([over_pixels(h) for h in hidden] * 4, axis=0), pix, group)
    centered = [h - mean[f : f + 1] for f, h in enumerate(hidden)]
    variance = group_mean(jnp.concatenate([over_pixels(v * v) for v in centered] * 4, axis=0), pix, group)
    inv_std = lax.rsqrt(variance + EPSILON)
    sums, kept = [], []
    for f in range(2):
        normed = centered[f] * inv_std[f : f + 1]
        preact = normed * gain + bias
        sig = jax.nn.sigmoid(preact)
        act_s[order[f]] = (preact * sig).T.astype(BF16)
        grad_pre = ga_s[f].astype(F32) * sig * (1.0 + preact * (1.0 - sig))
        grad_normed = grad_pre * gain
        sums += [over_pixels(grad_normed), over_pixels(grad_normed * normed)]
        kept.append((grad_normed, normed))
    means = group_mean(jnp.concatenate(sums * 2, axis=0), pix, group)
    for f, (grad_normed, normed) in enumerate(kept):
        mean_grad, mean_proj = means[2 * f : 2 * f + 1], means[2 * f + 1 : 2 * f + 2]
        gh_ref[f, :, :] = ((grad_normed - mean_grad - normed * mean_proj) * inv_std[f : f + 1]).astype(BF16)
    if len(act_refs) == 1:
        act_refs[0][...] = act_s[...]
    else:
        n = pix // len(act_refs)
        for s, out in enumerate(act_refs):
            for f in range(2):
                out[f, :, :] = act_s[f, :, pl.ds(pl.multiple_of(n * (z ^ s), n), n)]


def send_out(scratch, outs, x, y):
    a_keep, a_send, b_keep, b_send = outs
    for t in range(2):
        a_send[t] = scratch[0, (x ^ 1) + 2 * (y ^ t)]
        b_send[t] = scratch[1, (x ^ t) + 2 * (y ^ 1)]
        a_keep[t] = scratch[0, x + 2 * (y ^ t)]
        b_keep[t] = scratch[1, (x ^ t) + 2 * y]


def spatial_kernel(xt_ref, gh_ref, ak, asend, bk, bsend, p_s, *, cols, start, quarter):
    x, y, _, _ = place()
    _, pix, width = gh_ref.shape
    chans = xt_ref.shape[2]
    count = p_s.shape[2]
    for q in range(4):
        row = q * quarter + start
        stop = row + count
        while row < stop:
            tap, chan = divmod(row, chans)
            size = min(chans - chan, stop - row)
            a, b = divmod(tap, 3)
            lhs = slice(chan, chan + size)
            acc = dot(xt_ref[0, b, lhs, cols * a : cols * a + pix], gh_ref[0])
            acc += dot(xt_ref[1, b, lhs, cols * a : cols * a + pix], gh_ref[1])
            at = row - q * quarter - start
            p_s[0, q, at : at + size, :] = acc[:, : width // 2].astype(BF16)
            p_s[1, q, at : at + size, :] = acc[:, width // 2 :].astype(BF16)
            row += size
    send_out(p_s, (ak, asend, bk, bsend), x, y)


def time_kernel(*refs, parts, pixels):
    pieces, g_ref, outs, p_s, a_s = refs[:parts], refs[parts], refs[parts + 1 : parts + 5], refs[-2], refs[-1]
    x, y, z, _ = place()
    half, total = a_s.shape
    quarter = p_s.shape[2]
    block = half // 4
    for s, piece in enumerate(pieces):
        for f in range(2):
            lanes = pl.multiple_of(pixels * (2 * (z ^ s) + f), pixels)
            a_s[:, pl.ds(lanes, pixels)] = piece[f, :, :]
    for k in range(3):
        acc = dot(a_s[:, : total - pixels * k], g_ref[pixels * k :, :])
        for s in range(4):
            q, r = divmod(k * half + block * s, quarter)
            v = acc[block * s : block * (s + 1)].astype(BF16)
            p_s[0, q, r : r + block, :] = v[:, :half]
            p_s[1, q, r : r + block, :] = v[:, half:]
    send_out(p_s, outs, x, y)


def half_kernel(ak, ra, bk, rb, next_a, next_b):
    next_a[...] = (ak[1].astype(F32) + ra[1].astype(F32)).astype(BF16)
    next_b[...] = (bk[1].astype(F32) + rb[1].astype(F32)).astype(BF16)


def fold_kernel(ak, ra, r2a, bk, rb, r2b, *refs, packed):
    outs, v_s = refs[:4], refs[4]
    _, _, z, _ = place()
    rows, lanes = ak.shape[1:]
    h = rows // 2
    for t, (k, r, r2) in enumerate(((ak, ra, r2a), (bk, rb, r2b))):
        if packed:
            low = low_lanes((h, lanes))
            top, bot = (
                k[0, rr, :].astype(F32) + r[0, rr, :].astype(F32) + r2[rr, :].astype(F32) for rr in (slice(0, h), slice(h, rows))
            )
            v_s[2 * t] = jnp.where(low, top, swap(bot)).astype(BF16)
            v_s[2 * t + 1] = jnp.where(low, swap(top), bot).astype(BF16)
        else:
            v = k[0].astype(F32) + r[0].astype(F32) + r2[...].astype(F32)
            v_s[2 * t] = v[:, : lanes // 2].astype(BF16)
            v_s[2 * t + 1] = v[:, lanes // 2 :].astype(BF16)
    for s, out in enumerate(outs):
        out[...] = v_s[z ^ s]


def last_kernel(*refs, scale):
    out_ref, t_s = refs[-2:]
    row = 0
    for n in range(0, len(refs) - 2, 4):
        total = sum(ref[...].astype(F32) for ref in refs[n : n + 4]) * scale
        h = total.shape[0]
        t_s[row : row + h, :] = total
        t_s[row + h : row + 2 * h, :] = swap(total)
        row += 2 * h
    out_ref[...] = t_s[...].T[: out_ref.shape[0]]


def sum_kernel(a, b, c, d, out_ref, *, scale):
    out_ref[...] = (a[...].astype(F32) + b[...].astype(F32) + c[...].astype(F32) + d[...].astype(F32)) * scale


def join_kernel(own_ref, par_ref, out_ref, t_s):
    _, _, _, c = place()
    block = out_ref.shape[0]
    for core, ref in ((c, own_ref), (1 - c, par_ref)):
        v = ref[...]
        v = jnp.where(c == 0, v, swap(v))
        for n in range(v.shape[0] // block):
            t_s[pl.ds(pl.multiple_of(block * (2 * n + core), block), block), :] = v[block * n : block * (n + 1)]
    out_ref[...] = t_s[...].T[:block]


def clips_kernel(gh_ref, ws_ref, own_ref, par_ref, y_s, *, cols):
    _, pix, width = gh_ref.shape
    chans = own_ref.shape[1]
    for f, out in enumerate((own_ref, par_ref)):
        gh = gh_ref[f].astype(F32)
        for b in range(3):
            y_s[b, 0:cols, :] = jnp.zeros((cols, width), BF16)
            y_s[b, cols + pix :, :] = jnp.zeros((cols, width), BF16)
            y_s[b, cols : cols + pix, :] = shifted(gh, cols, 1 - b).astype(BF16)
        acc = None
        for a in range(3):
            for b in range(3):
                tap = 3 * a + b
                part = dot_nt(y_s[b, cols * (2 - a) : cols * (2 - a) + pix, :], ws_ref[chans * tap : chans * (tap + 1), :])
                acc = part if acc is None else acc + part
        out[...] = acc


def add_kernel(a, b, out_ref):
    out_ref[...] = (a[...] + b[...]).astype(BF16)


def call(kernel, outs, *args, scratch=(), name=None, local=True, final=False):
    near = (lambda v: pltpu.with_memory_space_constraint(v, pltpu.VMEM)) if local else (lambda v: v)
    return pl.pallas_call(
        kernel,
        out_shape=jax.tree.map(lambda v: pltpu.VMEM(v.shape, v.dtype), outs) if local and not final else outs,
        in_specs=[VM] * len(args),
        out_specs=jax.tree.map(lambda _: VM, outs),
        scratch_shapes=list(scratch),
        compiler_params=pltpu.CompilerParams(vmem_limit_bytes=SCOPED) if local else None,
        name=name,
    )(*(near(v) for v in args))


def send_dp(v, s):
    return lax.ppermute(v, "dp", [(i, i ^ s) for i in range(lax.axis_size("dp"))])


def send_wide(v, s):
    return lax.ppermute(v, "wide", [(i, i ^ s) for i in range(lax.axis_size("wide"))])


def z_groups():
    n = lax.axis_size("wide")
    return [list(range(0, n, 2)), list(range(1, n, 2))]


def over_z(v):
    return lax.all_to_all(v, "wide", 0, 0, tiled=True, axis_index_groups=z_groups())


def shards(clips, w_spatial, w_time, norm_gain, norm_bias, grad_out):
    group_count, frame_count, rows, cols, chans = clips.shape
    n_dp, n_wide = lax.axis_size("dp"), lax.axis_size("wide")
    chips = n_wide // 2
    assert group_count == 1 and frame_count == 1 and n_dp == 4
    pix = rows * cols
    half = chans // 2
    width = half // 4
    taps_rows = w_spatial.shape[0]
    _, frame_total, pix_here, _ = grad_out.shape
    pixels = 2 * pix_here
    small = chips == 4 and pixels % 128 == 0
    w = lax.axis_index("wide")
    c = w % 2

    run = functools.partial(call, local=small)

    pack = struct((taps_rows // 4, 2 * width), BF16)
    own_t, own_b = run(pack_kernel, (pack, pack), w_spatial, name="pack")
    x_t, y_b = send_dp(own_t, 1), send_dp(own_b, 2)
    x_b, y_t = send_dp(own_b, 1), send_dp(own_t, 2)
    d_t, d_b = send_dp(x_t, 2), send_dp(y_b, 1)

    own_clips = clips.reshape(pix, chans)
    own_go = grad_out[0]
    par_go = send_wide(own_go, 1)
    par_clips = send_wide(own_clips, 1)

    if small:
        pieces = (own_go, par_go)
        gact_out = (struct((2 * pixels, half), BF16),) * chips
    else:
        even, odd = jnp.where(c == 0, own_go, par_go), jnp.where(c == 0, par_go, own_go)
        pieces = (jnp.concatenate([even, odd], axis=1),)
        gact_out = (struct((frame_total * pixels, half), BF16),)
    *gact, go = run(
        functools.partial(gact_kernel, parts=len(pieces), pixels=pixels, chips=chips),
        (*gact_out, struct((frame_total * pixels, chans), BF16)),
        *pieces,
        w_time,
        scratch=(pltpu.VMEM((3, half, chans), BF16), pltpu.VMEM((frame_total * pixels, half), F32)),
        name="gact",
    )
    if small:
        gact = [gact[0]] + [send_wide(gact[s], 2 * s) for s in range(1, chips)]
    else:
        gact = over_z(gact[0].reshape(chips, 2, pixels, half)).transpose(1, 0, 2, 3).reshape(2, pix, half)
        gact = [gact]
    x3, xt = run(
        functools.partial(prep_kernel, cols=cols),
        (struct((2, pix + 2 * cols, 3 * chans), BF16), struct((2, 3, chans, pix + 2 * cols), BF16)),
        own_clips,
        par_clips,
        name="prep",
    )
    gain = norm_gain.reshape(n_dp, 2, width)
    bias = norm_bias.reshape(n_dp, 2, width)
    gain, bias = (lax.dynamic_index_in_dim(v, c, 1).reshape(1, half) for v in (gain, bias))
    act_out = (struct((2, half, pixels), BF16),) * chips if small else (struct((2, half, pix), BF16),)
    gh, ws, *act = run(
        functools.partial(main_kernel, cols=cols, group=chans // G, parts=len(gact)),
        (struct((2, pix, half), BF16), struct((taps_rows, half), BF16), *act_out),
        *(own_t, x_t, y_t, d_t, own_b, x_b, y_b, d_b, x3, *gact, gain, bias),
        scratch=(pltpu.VMEM((2, pix, half), BF16), pltpu.VMEM((2, pix, half), BF16), pltpu.VMEM((2, half, pix), BF16)),
        name="main",
    )

    position_total = group_count * frame_count * pix * n_wide * n_dp
    grad_scale = float(position_total) ** (-0.5)

    def reduce_dp(parts):
        a_keep, a_send, b_keep, b_send = parts
        ra, rb = send_dp(a_send, 1), send_dp(b_send, 2)
        out = struct(a_keep.shape[1:], BF16)
        next_a, next_b = run(half_kernel, (out, out), a_keep, ra, b_keep, rb, name="half")
        return a_keep, ra, send_dp(next_a, 2), b_keep, rb, send_dp(next_b, 1)

    def fold(parts, packed):
        count, lanes = parts[0].shape[1:]
        shape = (count // 2, lanes) if packed else (count, lanes // 2)
        chunks = run(
            functools.partial(fold_kernel, packed=packed),
            (struct(shape, BF16),) * 4,
            *parts,
            scratch=(pltpu.VMEM((4, *shape), BF16),),
            name="fold",
        )
        return [chunks[0]] + [send_wide(chunks[s], 2 * s) for s in range(1, 4)]

    def fold_apart(parts):
        a_keep, ra, r2a, b_keep, rb, r2b = parts
        total = jnp.concatenate(
            [k[0].astype(F32) + r[0].astype(F32) + r2.astype(F32) for k, r, r2 in ((a_keep, ra, r2a), (b_keep, rb, r2b))],
            axis=1,
        )
        count, columns = total.shape
        chunks = total.astype(BF16).reshape(count, chips, columns // chips).transpose(1, 0, 2)
        return jnp.sum(over_z(chunks).astype(F32), axis=0) * grad_scale

    quarter = taps_rows // n_dp
    n_pieces = PIECES
    count = quarter // n_pieces
    spatial = []
    for h in range(n_pieces):
        out = struct((2, count, half // 2), BF16)
        spatial.append(
            reduce_dp(
                run(
                    functools.partial(spatial_kernel, cols=cols, start=h * count, quarter=quarter),
                    (out,) * 4,
                    xt,
                    gh,
                    scratch=(pltpu.VMEM((2, n_dp, count, half // 2), BF16),),
                    name="spatial",
                )
            )
        )

    t_quarter = w_time.shape[0] // n_dp
    out = struct((2, t_quarter // 2, half), BF16)
    if small:
        act = [act[0]] + [send_wide(act[s], 2 * s) for s in range(1, chips)]
        timed = run(
            functools.partial(time_kernel, parts=chips, pixels=pixels),
            (out,) * 4,
            *act,
            go,
            scratch=(pltpu.VMEM((2, n_dp, t_quarter // 2, half), BF16), pltpu.VMEM((half, frame_total * pixels), BF16)),
            name="time",
        )
    else:
        moved = act[0].reshape(2, half, chips, pixels).transpose(2, 0, 1, 3)
        moved = over_z(moved).reshape(-1, FRAMES, half, pixels)
        later = go.reshape(-1, FRAMES, pixels, chans)
        taps = [
            jnp.einsum("nfcp,nfpo->co", moved[:, : FRAMES - k], later[:, k:], preferred_element_type=F32) for k in range(3)
        ]
        quarters = jnp.concatenate(taps, axis=0).astype(BF16).reshape(n_dp, t_quarter // 2, 2, half)
        dp = lax.axis_index("dp")
        pick = lambda s, t: lax.dynamic_index_in_dim(quarters, dp ^ s, 0, False)[:, t]
        timed = [jnp.stack([pick(s, t), pick(r, t)]) for s, r, t in ((0, 2, 0), (1, 3, 0), (0, 1, 1), (2, 3, 1))]
    timed = reduce_dp(timed)

    image = struct((pix, chans), F32)
    own_grad, par_grad = run(
        functools.partial(clips_kernel, cols=cols),
        (image, image),
        gh,
        ws,
        scratch=(pltpu.VMEM((3, pix + 2 * cols, half), BF16),),
        name="clips",
    )
    grad_clips = run(add_kernel, struct((pix, chans), BF16), own_grad, send_wide(par_grad, 1), name="add", final=True)
    grad_clips = grad_clips.reshape(clips.shape)

    if small:
        got = [v for part in spatial for v in fold(part, True)]
        spatial_grad = run(
            functools.partial(last_kernel, scale=grad_scale),
            struct((width, quarter), F32),
            *got,
            scratch=(pltpu.VMEM((quarter, 2 * width), F32),),
            name="last",
            final=True,
        ).T
        mine = run(
            functools.partial(sum_kernel, scale=grad_scale),
            struct((t_quarter // 2, 2 * width), F32),
            *fold(timed, False),
            name="sum",
        )
        time_grad = run(
            join_kernel,
            struct((width, t_quarter), F32),
            mine,
            send_wide(mine, 1),
            scratch=(pltpu.VMEM((t_quarter, 2 * width), F32),),
            name="join",
            final=True,
        ).T
        return grad_clips, spatial_grad, time_grad

    block = half // chips
    mine = jnp.concatenate([fold_apart(part) for part in spatial], axis=0)
    moves = []
    for src in range(n_wide):
        s, i = divmod((src // 2) * block, width)
        moves.append((src, (2 * width * s + width * (src % 2) + i) // block))
    spatial_grad = lax.ppermute(mine, "wide", moves)
    mine = fold_apart(timed)
    other = send_wide(mine, 1)
    even, odd = jnp.where(c == 0, mine, other), jnp.where(c == 0, other, mine)
    joined = jnp.stack([v.reshape(-1, width, 2, block) for v in (even, odd)], axis=1)
    time_grad = lax.dynamic_index_in_dim(joined, c, 3, False).reshape(t_quarter, block)
    return grad_clips, spatial_grad, time_grad


def solution(mesh):
    return jax.shard_map(
        shards,
        mesh=mesh,
        in_specs=(
            P("dp", "wide", None, None, None),
            P(None, "dp"),
            P(),
            P(),
            P(),
            P("dp", None, "wide", None),
        ),
        out_specs=(P("dp", "wide", None, None, None), P("dp", "wide"), P("dp", "wide")),
        check_vma=False,
    )
```
